32 devices in a mesh: row: 4 (over z), col: 8 (over y, x, core).
Axes of the slice: x: 2, y: 2, z: 4, core: 2. Of those that a mesh axis runs over, the one named last changes fastest.
Arguments:
- panel_block: float32 [512, 512], P(('row', 'col')), may hold values from -1 to 10, as said below
- panel_cross: float32 [8192, 512], P('col'), may hold values from -0.375 to 0.375
- trail_block: float32 [8192, 8192], P('row', 'col'), may hold values from -1.2 to 1.2
- panel_pixels: float32 [512, 16384], P('row', 'col'), may hold values from -0.375 to 0.375
- trail_pixels: float32 [8192, 16384], P('row', 'col'), may hold values from -1.2 to 1.2
- panel_sectors: float32 [512, 1024], P('row'), may hold values from -6 to 6
- trail_sectors: float32 [8192, 1024], P('col', 'row'), may hold values from -1.2 to 1.2
Outputs:
- panel_factor: float32 [512, 512], P(('row', 'col'))
- panel_columns: float32 [8192, 512], P('col')
- trail_updated: float32 [8192, 8192], P('row', 'col')
- pixels_updated: float32 [8192, 16384], P('row', 'col')
- sectors_updated: float32 [8192, 1024], P('col', 'row')
- prediction: float32 [16384, 1024], P('col', 'row')
The draws below stay inside these ranges and needn't reach their ends.
Inputs may be any that keep to these rules, and one draw needn't show every extreme that they name: `panel_block`: symmetric positive definite.
All inputs are finite; a program needn't handle non-finite values.
Results may differ from the reference program's by a relative error of at most 0.000075.
Values sent between devices are 32-bit elements; how exact they have to be, the bound alone decides.
No kernel may reach another device: no remote copies, remote signals or barrier semaphores. Data moves between devices by JAX's collectives and lax.ppermute only.
A program may use at most 128 MiB of HBM per device.

```python
import jax
import jax.numpy as jnp
from jax import lax

PANEL = 256
PW = 512
TRAIL = 8192
PIXELS = 16384
SECTORS = 1024


def draw_panel_block(key, part):
    first_key, second_key = jax.random.split(jax.random.fold_in(key, 11))
    raw = jax.random.normal(first_key, (PW, PW), jnp.float32)
    scales = jnp.exp(jax.random.uniform(second_key, (PW,), jnp.float32, 0.0, 1.3862944))
    product = jnp.dot(raw, raw.T, precision=lax.Precision.HIGHEST)
    return 0.5 * product / PW + jnp.diag(scales)


def steps_of(own_key, extent, cuts, least, top_value):
    gain = 1.0
    for dim, blocks in cuts:
        heights = jax.random.uniform(jax.random.fold_in(jax.random.fold_in(own_key, 6), dim), (blocks,), jnp.float32, least / len(cuts), top_value / len(cuts))
        gain = gain * jnp.repeat(jnp.exp(heights), extent[dim] // blocks).reshape((-1,) + (1,) * (len(extent) - 1 - dim))
    return gain


def normal_values(rng, extent, scale, limit, pieces=(), held_as=jnp.bfloat16):
    result = scale * jax.random.normal(rng, extent, jnp.float32)
    if pieces:
        result = result * steps_of(rng, extent, pieces, -0.22, 0.18)
    return jnp.clip(result, -limit, limit).astype(held_as)


def setup_inputs(seed: int = 0) -> dict:
    streams_of = jax.random.split(jax.random.key(seed), 8)
    return {
        "panel_block": draw_panel_block(jax.random.fold_in(streams_of[7], 71), 0),
        "panel_cross": normal_values(streams_of[1], (TRAIL, PW), PANEL ** -0.5, 0.375, ((0, 8),), jnp.float32),
        "trail_block": normal_values(streams_of[2], (TRAIL, TRAIL), 0.2, 1.2, ((0, 4), (1, 8)), jnp.float32),
        "panel_pixels": normal_values(streams_of[3], (PW, PIXELS), PANEL ** -0.5, 0.375, ((0, 4), (1, 8)), jnp.float32),
        "trail_pixels": normal_values(streams_of[4], (TRAIL, PIXELS), 0.2, 1.2, ((0, 4), (1, 8)), jnp.float32),
        "panel_sectors": normal_values(streams_of[5], (PW, SECTORS), 1.0, 6.0, ((0, 4),), jnp.float32),
        "trail_sectors": normal_values(streams_of[6], (TRAIL, SECTORS), 0.2, 1.2, ((0, 8), (1, 4)), jnp.float32),
    }


def reference(panel_block, panel_cross, trail_block, panel_pixels, trail_pixels, panel_sectors, trail_sectors):
    highest = lax.Precision.HIGHEST
    factor = jnp.linalg.cholesky(panel_block)
    columns = lax.linalg.triangular_solve(factor, panel_cross, left_side=False, lower=True, transpose_a=True)
    trail_updated = trail_block - lax.dot_general(columns, columns, (((1,), (1,)), ((), ())), precision=highest)
    solved = lax.linalg.triangular_solve(factor, panel_sectors, left_side=True, lower=True)
    kriging_weights = lax.linalg.triangular_solve(factor, solved, left_side=True, lower=True, transpose_a=True)
    sectors_updated = trail_sectors - jnp.dot(columns, solved, precision=highest)
    coupling = lax.linalg.triangular_solve(factor, columns, left_side=False, lower=True)
    pixels_updated = trail_pixels - jnp.dot(coupling, panel_pixels, precision=highest)
    prediction = lax.dot_general(panel_pixels, kriging_weights, (((0,), (0,)), ((), ())), precision=highest)
    return (factor, columns, trail_updated, pixels_updated, sectors_updated, prediction)
```

```python
import jax
import jax.numpy as jnp
from jax import lax
from jax.experimental import pallas as pl
from jax.experimental.pallas import tpu as pltpu
from jax.sharding import PartitionSpec as P


HIGHEST = lax.Precision.HIGHEST
LANES = 128
SUBLANES = 8
COLUMN_STEPS = 4


def invert_block(tiles):
    count = len(tiles)
    width = tiles[0].shape[1]
    shape = (SUBLANES, width)
    lane = lax.broadcasted_iota(jnp.int32, shape, 1)
    sub = lax.broadcasted_iota(jnp.int32, shape, 0)

    def lanes_of(x, j):
        return jnp.broadcast_to(x[:, j : j + 1], shape)

    def row_of(x, i):
        return jnp.broadcast_to(x[i : i + 1, :], shape)

    m = list(tiles)
    out = []
    for g in range(count):
        base = SUBLANES * g
        inside = (lane >= base) & (lane < base + SUBLANES)
        columns = [[lanes_of(m[v], base + q) for q in range(SUBLANES)] for v in range(g, count)]
        s = [
            [row_of(columns[0][q], i) if i >= q else None for q in range(SUBLANES)]
            for i in range(SUBLANES)
        ]
        low = [[None] * SUBLANES for _ in range(SUBLANES)]
        pivot_inv = []
        root_inv = []
        for q in range(SUBLANES):
            pivot_inv.append(1.0 / s[q][q])
            root_inv.append(lax.rsqrt(s[q][q]))
            for i in range(q + 1, SUBLANES):
                low[i][q] = s[i][q] * pivot_inv[q]
            for i in range(q + 1, SUBLANES):
                for k in range(q + 1, i + 1):
                    s[i][k] = s[i][k] - low[i][q] * s[k][q]
        rows = []
        for q in range(SUBLANES):
            x = jnp.where(inside, jnp.where(lane == base + q, 1.0, 0.0), row_of(m[g], q))
            for p in range(q):
                x = x - low[q][p] * rows[p]
            rows.append(x)
        own = jnp.zeros(shape, jnp.float32)
        for q in range(SUBLANES):
            own = jnp.where((sub == q) & (lane <= base + q), rows[q] * root_inv[q], own)
        out.append(own)
        for v in range(g + 1, count):
            done = []
            for q in range(SUBLANES):
                x = columns[v - g][q]
                for p in range(q):
                    x = x - done[p] * low[q][p]
                done.append(x)
            x = jnp.where(inside, 0.0, m[v])
            for q in range(SUBLANES):
                x = x - (done[q] * pivot_inv[q]) * rows[q]
            m[v] = x
    return out


def factor_step(k, m_ref, l_ref, wk_ref):
    size = m_ref.shape[0]
    width = wk_ref.shape[0]
    offset = k * width if isinstance(k, int) else pl.multiple_of(k * width, width)
    span = pl.ds(offset, width)
    block = m_ref.at[span, span]
    tiles = [block[i : i + SUBLANES, :] for i in range(0, width, SUBLANES)]
    for i, tile in enumerate(invert_block(tiles)):
        wk_ref[i * SUBLANES : (i + 1) * SUBLANES, :] = tile
    inverse = wk_ref[...]
    panel = lax.dot_general(
        m_ref[:, span],
        inverse,
        (((1,), (1,)), ((), ())),
        precision=HIGHEST,
        preferred_element_type=jnp.float32,
    )
    row = lax.broadcasted_iota(jnp.int32, (size, width), 0)
    col = lax.broadcasted_iota(jnp.int32, (size, width), 1) + offset
    below = row >= offset + width
    l_ref[:, span] = jnp.where(row >= col, panel, 0.0)
    ii = lax.broadcasted_iota(jnp.int32, (width, width), 0)
    jj = lax.broadcasted_iota(jnp.int32, (width, width), 1)
    m_ref[span, span] = jnp.where(ii == jj, 1.0, 0.0)
    upper = jnp.dot(inverse, m_ref[span, :], precision=HIGHEST, preferred_element_type=jnp.float32)
    lane = lax.broadcasted_iota(jnp.int32, (width, size), 1)
    m_ref[:, span] = jnp.where(below, 0.0, m_ref[:, span])
    m_ref[...] = m_ref[...] - jnp.dot(
        jnp.where(below, panel, 0.0),
        upper,
        precision=HIGHEST,
        preferred_element_type=jnp.float32,
    )
    m_ref[span, :] = jnp.where(lane < offset + width, upper, 0.0)


def first_kernel(place_ref, *refs):
    pieces, (l_ref, m_ref, wk_ref) = refs[:-3], refs[-3:]
    n_row, count, _ = pieces[0].shape
    for t, piece in enumerate(pieces):
        for m in range(n_row):
            slot = (place_ref[0] ^ m) * len(pieces) + (place_ref[1] ^ t)
            m_ref[pl.ds(pl.multiple_of(slot * count, count), count), :] = piece[m]
    l_ref[...] = jnp.zeros_like(l_ref)

    @pl.loop(0, m_ref.shape[0] // wk_ref.shape[0] // 2)
    def _(k):
        factor_step(k, m_ref, l_ref, wk_ref)


def second_kernel(l_in, m_in, l_ref, m_ref, wk_ref):
    l_ref[...] = l_in[...]
    m_ref[...] = m_in[...]
    blocks = m_ref.shape[0] // wk_ref.shape[0]

    @pl.loop(blocks // 2, blocks - 1)
    def _(k):
        factor_step(k, m_ref, l_ref, wk_ref)


def third_kernel(place_ref, l_in, m_in, c_ref, *refs):
    results, refs = refs[:6], refs[6:]
    stores, (l_ref, m_ref, wk_ref, sems) = refs[:6], refs[6:]
    rows_out, o_ref, oh, ol, wh, wl = stores
    l_ref[...] = l_in[...]
    m_ref[...] = m_in[...]
    blocks = m_ref.shape[0] // wk_ref.shape[0]

    factor_step(blocks - 1, m_ref, l_ref, wk_ref)
    count = rows_out.shape[0]
    if count == l_ref.shape[0]:
        rows_out[...] = l_ref[...]
    else:
        rows_out[...] = l_ref[pl.ds(pl.multiple_of(place_ref[0] * count, count), count), :]
    wh[...], wl[...] = split(m_ref[...])
    copies = []

    def send(i, span):
        copy = pltpu.make_async_copy(
            stores[i].at[span], results[i].at[span], sems.at[len(copies)]
        )
        copy.start()
        copies.append(copy)

    for i in (0, 4, 5):
        send(i, pl.ds(0, stores[i].shape[0]))
    step = c_ref.shape[0] // COLUMN_STEPS
    for t in range(COLUMN_STEPS):
        span = pl.ds(t * step, step)
        out = lower_nt(split(c_ref[span, :]), (wh, wl))
        o_ref[span, :] = out
        oh[span, :], ol[span, :] = split(out)
        for i in (1, 2, 3):
            send(i, span)
    for copy in copies:
        copy.wait()


def factor_parts(size):
    square = shape(size, size)
    scratch = [pltpu.VMEM((LANES, LANES), jnp.float32)]
    vmem = pl.BlockSpec(memory_space=pltpu.VMEM)
    smem = pl.BlockSpec(memory_space=pltpu.SMEM)

    def first(place, pieces):
        return pl.pallas_call(
            first_kernel,
            out_shape=(square, square),
            in_specs=[smem] + [vmem] * len(pieces),
            out_specs=(vmem, vmem),
            scratch_shapes=scratch,
            name="factor_first",
        )(place, *pieces)

    def second(low, m):
        return pl.pallas_call(
            second_kernel,
            out_shape=(square, square),
            in_specs=[vmem, vmem],
            out_specs=(vmem, vmem),
            scratch_shapes=scratch,
            name="factor_second",
        )(low, m)

    def third(place, low, m, cross, count):
        rows = cross.shape[0]
        results = (
            (shape(count, size), shape(rows, size))
            + pair_shape(rows, size)
            + pair_shape(size, size)
        )
        return pl.pallas_call(
            third_kernel,
            out_shape=results,
            in_specs=[smem, vmem, vmem, vmem],
            out_specs=(pl.BlockSpec(memory_space=pltpu.HBM),) * len(results),
            scratch_shapes=[pltpu.VMEM(x.shape, x.dtype) for x in results]
            + [pltpu.VMEM((size, size), jnp.float32)] * 2
            + scratch
            + [pltpu.SemaphoreType.DMA((3 + 3 * COLUMN_STEPS,))],
            name="factor_third",
        )(place, low, m, cross)

    return first, second, third


NT = ((1,), (1,))
NN = ((1,), (0,))
TN = ((0,), (0,))


def split(x):
    high = x.astype(jnp.bfloat16)
    return high, (x - high.astype(jnp.float32)).astype(jnp.bfloat16)


def product(a, b, dims):
    def one(x, y):
        return lax.dot_general(x, y, (dims, ((), ())), preferred_element_type=jnp.float32)

    return one(a[0], b[0]) + (one(a[0], b[1]) + one(a[1], b[0]))


def shape(*dims, dtype=jnp.float32):
    return jax.ShapeDtypeStruct(dims, dtype)


def pair_shape(*dims):
    return (shape(*dims, dtype=jnp.bfloat16),) * 2


def in_hbm(x):
    return pltpu.with_memory_space_constraint(x, pltpu.HBM)


def full(*dims):
    return pl.BlockSpec(dims, lambda i, *_: (0,) * len(dims))


def tiles(*dims):
    return pl.BlockSpec(dims, lambda i, *_: (i,) + (0,) * (len(dims) - 1))


def run(kernel, grid, in_specs, out_specs, out_shape, scratch=(), prefetch=0, alias={}):
    return pl.pallas_call(
        kernel,
        grid_spec=pltpu.PrefetchScalarGridSpec(
            num_scalar_prefetch=prefetch,
            grid=(grid,),
            in_specs=in_specs,
            out_specs=out_specs,
            scratch_shapes=list(scratch),
        ),
        out_shape=out_shape,
        input_output_aliases=alias,
        compiler_params=pltpu.CompilerParams(vmem_limit_bytes=48 << 20),
    )


def lower_nt(x, w_refs):
    pw = w_refs[0].shape[0]
    h = pw // 2
    top = product((x[0][:, :h], x[1][:, :h]), tuple(w[:h, :h] for w in w_refs), NT)
    low = product(x, tuple(w[h:, :] for w in w_refs), NT)
    return jnp.concatenate([top, low], 1)


def lower_nn(x, w_refs):
    pw = w_refs[0].shape[0]
    h = pw // 2
    left = product(x, tuple(w[:, :h] for w in w_refs), NN)
    right = product((x[0][:, h:], x[1][:, h:]), tuple(w[h:, h:] for w in w_refs), NN)
    return jnp.concatenate([left, right], 1)


def placed(flag_ref, masks, refs, out_refs):
    for m, x in zip(masks, refs):
        if isinstance(x, tuple):
            value = jnp.where(flag_ref[2] != 0, x[0][...], x[1][...])
        else:
            value = x[...]
        size = value.shape[0]
        span = pl.ds(pl.multiple_of((flag_ref[0] ^ m) * size, size), size)
        for out, part in zip(out_refs, split(value)):
            out[span, :] = part


def rows(picks, crosses, inverse, own, trail, tile):
    count, pw = crosses[0].shape
    total, width = trail.shape
    steps = count // tile

    def kernel(pick_ref, *refs):
        choices, (wh, wl, oh, ol, t_ref, out_ref, ch_ref, cl_ref) = (
            refs[: len(crosses)],
            refs[len(crosses) :],
        )
        pick = pick_ref[pl.program_id(0) // steps]
        x = choices[0][...]
        for i in range(1, len(choices)):
            x = jnp.where(pick == i, choices[i][...], x)
        r = split(lower_nt(split(x), (wh, wl)))
        out_ref[...] = t_ref[...] - product(r, (oh[...], ol[...]), NT)
        ch_ref[...], cl_ref[...] = split(lower_nn(r, (wh, wl)))

    side = pl.BlockSpec((tile, pw), lambda i, p: (i % steps, 0))
    return run(
        kernel,
        total // tile,
        [side] * len(crosses)
        + [full(pw, pw)] * 2
        + [full(*own[0].shape)] * 2
        + [tiles(tile, width)],
        (tiles(tile, width), tiles(tile, pw), tiles(tile, pw)),
        (shape(total, width),) + (pltpu.HBM((total, pw), jnp.bfloat16),) * 2,
        prefetch=1,
    )(picks, *crosses, *inverse, *own, trail)


def flatten(pieces):
    return [x for p in pieces for x in (p if isinstance(p, tuple) else (p,))]


def regroup(pieces, refs):
    it = iter(refs)
    return [(next(it), next(it)) if isinstance(p, tuple) else next(it) for p in pieces]


def maps(flags, masks, pieces, sectors, inverse, own, coupling, base, trail, tile):
    total, width = base.shape
    arrays = flatten(pieces)
    pw = inverse[0].shape[0]
    steps = total // tile
    own_rows, own_width = trail.shape
    own_tile, cut = own_rows // steps, width // steps
    n, k = len(arrays), len(sectors)

    def kernel(flag_ref, *refs):
        parts, sector_parts, refs = refs[:n], refs[n : n + k], refs[n + k :]
        wh, wl, oh, ol, ch, cl, b_ref, t_ref = refs[:8]
        out_ref, sec_ref, pred_ref, ph, plow, sh, sl, kh, kl = refs[8:]
        i = pl.program_id(0)

        @pl.when(i == 0)
        def _():
            placed(flag_ref, masks, regroup(pieces, parts), (ph, plow))
            placed(flag_ref, masks, sector_parts, (sh, sl))
            pair = (wh[...], wl[...])
            solved = split(product(pair, (sh[...], sl[...]), NN))
            sh[...], sl[...] = solved
            kh[...], kl[...] = split(product(pair, solved, TN))

        out_ref[...] = b_ref[...] - product((ch[...], cl[...]), (ph[...], plow[...]), NN)
        sec_ref[...] = t_ref[...] - product((oh[...], ol[...]), (sh[...], sl[...]), NN)
        span = pl.ds(pl.multiple_of(i * cut, cut), cut)
        pred_ref[...] = product((ph[:, span], plow[:, span]), (kh[...], kl[...]), TN)

    return run(
        kernel,
        steps,
        [full(*x.shape) for x in arrays + list(sectors)]
        + [full(pw, pw)] * 2
        + [tiles(own_tile, pw)] * 2
        + [tiles(tile, pw)] * 2
        + [tiles(tile, width), tiles(own_tile, own_width)],
        (tiles(tile, width), tiles(own_tile, own_width), tiles(cut, own_width)),
        (shape(total, width), shape(own_rows, own_width), shape(width, own_width)),
        scratch=[pltpu.VMEM((pw, width), jnp.bfloat16)] * 2
        + [pltpu.VMEM((pw, own_width), jnp.bfloat16)] * 4,
        prefetch=1,
    )(flags, *arrays, *sectors, *inverse, *own, *coupling, base, trail)


def exchange(x, axis, size, mask):
    return lax.ppermute(x, axis, [(i, i ^ mask) for i in range(size)])


def update(
    panel_block, panel_cross, trail_block, panel_pixels, trail_pixels, panel_sectors, trail_sectors
):
    n_row = lax.axis_size("row")
    n_col = lax.axis_size("col")
    r = lax.axis_index("row")
    c = lax.axis_index("col")
    count, pw = panel_block.shape
    owners = n_col // n_row
    first, second, third = factor_parts(pw)
    forward = n_row == 4
    masks = [0, 2, 1, 3] if forward else list(range(n_row))

    stack = [panel_block] + [exchange(panel_block, "row", n_row, m) for m in range(1, n_row)]
    stack = jnp.stack(stack)
    even = [stack] + [exchange(stack, "col", n_col, m) for m in range(2, n_col, 2)]
    odd = [exchange(x, "col", n_col, 1) for x in even]
    pieces = [x for pair in zip(even, odd) for x in pair]
    if count % SUBLANES:
        whole = jnp.stack(pieces)[jnp.arange(n_col) ^ c][:, jnp.arange(n_row) ^ r]
        whole = whole.transpose(1, 0, 2, 3).reshape(1, 1, pw, pw)
        pieces = [whole[0]]
        place = jnp.zeros((2,), jnp.int32)
    else:
        place = jnp.stack([r, c]).astype(jnp.int32)

    width = panel_sectors.shape[1] // n_row
    cut = lambda m: lax.dynamic_slice_in_dim(panel_sectors, (r ^ m) * width, width, 1)
    sector_pieces = [exchange(cut(m), "row", n_row, m) if m else cut(m) for m in masks]
    if forward:
        two = exchange(panel_pixels, "row", n_row, 2)
        near = exchange(panel_pixels, "row", n_row, 1)
        middle = lax.ppermute(panel_pixels, "row", [(1, 2), (2, 1)])
    else:
        pixel_pieces = [
            exchange(panel_pixels, "row", n_row, m) if m else panel_pixels for m in masks
        ]

    low, m = first(place, pieces)
    bits = n_col.bit_length() - 1
    parity = c % 2
    held = panel_cross
    orders = [[1 + (s + j) % (bits - 1) for s in range(bits - 1)] for j in range(owners)]
    reached = [[0] for _ in range(owners)]
    early = bits == 3
    for s in range(bits - 1):
        pairs = []
        receives = jnp.zeros((), jnp.bool_)
        for j in range(owners):
            bit = 1 << orders[j][s]
            for i in range(n_row):
                base = i * owners + j
                pairs += [(i * n_col + (base ^ x), i * n_col + (base ^ x ^ bit)) for x in reached[j]]
            for x in reached[j]:
                receives |= c == ((r * owners + j) ^ x ^ bit)
            reached[j] += [x ^ bit for x in reached[j]]
        got = lax.ppermute(held, ("row", "col"), pairs)
        if early and s == bits - 2:
            break
        held = jnp.where(receives, got, held)
    if early:
        beside = exchange(held, "col", n_col, 1)
        last = exchange(got, "col", n_col, 1)
        seat = c ^ (r * owners)
        source = seat < 2
        holder = source | (seat == (1 << orders[0][0])) | (seat == ((1 << orders[1][0]) | 1))
        mate = (seat == ((1 << orders[0][0]) | 1)) | (seat == (1 << orders[1][0]))
        crosses = [held, beside, got, last]
        kept = jnp.where(holder, 0, 2)
        swapped = jnp.where(source, 1, jnp.where(mate, 1, 3))
    else:
        crosses = [held, exchange(held, "col", n_col, 1)]
        kept, swapped = 0 * c, 0 * c + 1
    ints = lambda *v: jnp.stack([jnp.asarray(x, jnp.int32) for x in v])
    picks = ints(
        jnp.where(parity == 0, kept, swapped),
        jnp.where(parity == 0, swapped, kept),
    )

    whole_rows = count % SUBLANES != 0
    low, m = second(low, m)
    if forward:
        far = lax.ppermute(two, "row", [(1, 0), (2, 3)])
        pixel_pieces = [panel_pixels, two, near, (middle, far)]
    factor_rows, column_own, *pairs = third(
        ints(r * n_col + c), low, m, panel_cross, pw if whole_rows else count
    )
    pairs = [in_hbm(x) for x in pairs]
    own, inverse = pairs[0:2], pairs[2:4]
    if whole_rows:
        factor_rows = lax.dynamic_slice_in_dim(factor_rows, (r * n_col + c) * count, count, 0)
    tile = min(512, panel_cross.shape[0])
    trail_updated, *coupling = rows(picks, crosses, inverse, own, trail_block, tile)
    coupling = [in_hbm(x) for x in coupling]
    flags = ints(r, 0, (r == 1) | (r == 2))
    pixel_total, sectors_updated, predicted = maps(
        flags, masks, pixel_pieces, sector_pieces, inverse, own, coupling,
        trail_pixels, trail_sectors, tile,
    )
    return (factor_rows, column_own, trail_updated, pixel_total, sectors_updated, predicted)


def solution(mesh):
    return jax.shard_map(
        update,
        mesh=mesh,
        in_specs=(
            P(("row", "col"), None),
            P("col", None),
            P("row", "col"),
            P("row", "col"),
            P("row", "col"),
            P("row", None),
            P("col", "row"),
        ),
        out_specs=(
            P(("row", "col"), None),
            P("col", None),
            P("row", "col"),
            P("row", "col"),
            P("col", "row"),
            P("col", "row"),
        ),
        check_vma=False,
    )
```

```python
import jax
import jax.numpy as jnp
from jax import lax
from jax.experimental import pallas as pl
from jax.experimental.pallas import tpu as pltpu
from jax.sharding import PartitionSpec as P


HIGHEST = lax.Precision.HIGHEST
LANES = 128
SUBLANES = 8


def invert_block(tiles):
    count = len(tiles)
    width = tiles[0].shape[1]
    shape = (SUBLANES, width)
    lane = lax.broadcasted_iota(jnp.int32, shape, 1)
    sub = lax.broadcasted_iota(jnp.int32, shape, 0)

    def lanes_of(x, j):
        return jnp.broadcast_to(x[:, j : j + 1], shape)

    def row_of(x, i):
        return jnp.broadcast_to(x[i : i + 1, :], shape)

    m = list(tiles)
    out = []
    for g in range(count):
        base = SUBLANES * g
        inside = (lane >= base) & (lane < base + SUBLANES)
        columns = [[lanes_of(m[v], base + q) for q in range(SUBLANES)] for v in range(g, count)]
        s = [
            [row_of(columns[0][q], i) if i >= q else None for q in range(SUBLANES)]
            for i in range(SUBLANES)
        ]
        low = [[None] * SUBLANES for _ in range(SUBLANES)]
        pivot_inv = []
        root_inv = []
        for q in range(SUBLANES):
            pivot_inv.append(1.0 / s[q][q])
            root_inv.append(lax.rsqrt(s[q][q]))
            for i in range(q + 1, SUBLANES):
                low[i][q] = s[i][q] * pivot_inv[q]
            for i in range(q + 1, SUBLANES):
                for k in range(q + 1, i + 1):
                    s[i][k] = s[i][k] - low[i][q] * s[k][q]
        rows = []
        for q in range(SUBLANES):
            x = jnp.where(inside, jnp.where(lane == base + q, 1.0, 0.0), row_of(m[g], q))
            for p in range(q):
                x = x - low[q][p] * rows[p]
            rows.append(x)
        own = jnp.zeros(shape, jnp.float32)
        for q in range(SUBLANES):
            own = jnp.where((sub == q) & (lane <= base + q), rows[q] * root_inv[q], own)
        out.append(own)
        for v in range(g + 1, count):
            done = []
            for q in range(SUBLANES):
                x = columns[v - g][q]
                for p in range(q):
                    x = x - done[p] * low[q][p]
                done.append(x)
            x = jnp.where(inside, 0.0, m[v])
            for q in range(SUBLANES):
                x = x - (done[q] * pivot_inv[q]) * rows[q]
            m[v] = x
    return out


def factor_step(k, m_ref, l_ref, wk_ref):
    size = m_ref.shape[0]
    width = wk_ref.shape[0]
    offset = k * width if isinstance(k, int) else pl.multiple_of(k * width, width)
    span = pl.ds(offset, width)
    block = m_ref.at[span, span]
    tiles = [block[i : i + SUBLANES, :] for i in range(0, width, SUBLANES)]
    for i, tile in enumerate(invert_block(tiles)):
        wk_ref[i * SUBLANES : (i + 1) * SUBLANES, :] = tile
    inverse = wk_ref[...]
    start = offset if isinstance(k, int) else 0
    panel = lax.dot_general(
        m_ref[start:, span],
        inverse,
        (((1,), (1,)), ((), ())),
        precision=HIGHEST,
        preferred_element_type=jnp.float32,
    )
    row = lax.broadcasted_iota(jnp.int32, (size - start, width), 0) + start
    col = lax.broadcasted_iota(jnp.int32, (size - start, width), 1) + offset
    below = row >= offset + width
    l_ref[start:, span] = jnp.where(row >= col, panel, 0.0)
    ii = lax.broadcasted_iota(jnp.int32, (width, width), 0)
    jj = lax.broadcasted_iota(jnp.int32, (width, width), 1)
    m_ref[span, span] = jnp.where(ii == jj, 1.0, 0.0)
    upper = jnp.dot(inverse, m_ref[span, :], precision=HIGHEST, preferred_element_type=jnp.float32)
    lane = lax.broadcasted_iota(jnp.int32, (width, size), 1)
    if isinstance(k, int):
        start += width
        panel = panel[width:, :]
        m_ref[:, span] = jnp.zeros((size, width), jnp.float32)
    else:
        m_ref[:, span] = jnp.where(below, 0.0, m_ref[:, span])
        panel = jnp.where(below, panel, 0.0)
    if start < size:
        m_ref[start:, :] = m_ref[start:, :] - jnp.dot(
            panel, upper, precision=HIGHEST, preferred_element_type=jnp.float32
        )
    m_ref[span, :] = jnp.where(lane < offset + width, upper, 0.0)


def first_kernel(place_ref, *refs):
    pieces, (l_ref, m_ref, wk_ref) = refs[:-3], refs[-3:]
    n_row, count, _ = pieces[0].shape
    for t, piece in enumerate(pieces):
        for m in range(n_row):
            slot = (place_ref[0] ^ m) * len(pieces) + (place_ref[1] ^ t)
            m_ref[pl.ds(pl.multiple_of(slot * count, count), count), :] = piece[m]
    l_ref[...] = jnp.zeros_like(l_ref)

    @pl.loop(0, m_ref.shape[0] // wk_ref.shape[0] // 2)
    def _(k):
        factor_step(k, m_ref, l_ref, wk_ref)


def second_kernel(l_in, m_in, l_ref, m_ref, wk_ref):
    l_ref[...] = l_in[...]
    m_ref[...] = m_in[...]
    blocks = m_ref.shape[0] // wk_ref.shape[0]

    for k in range(blocks // 2, blocks - 1):
        factor_step(k, m_ref, l_ref, wk_ref)


def third_kernel(place_ref, l_in, m_in, *refs):
    results, (rows_out, wh, wl), (l_ref, m_ref, wk_ref, sems) = refs[:3], refs[3:6], refs[6:]
    l_ref[...] = l_in[...]
    m_ref[...] = m_in[...]
    factor_step(m_ref.shape[0] // wk_ref.shape[0] - 1, m_ref, l_ref, wk_ref)
    count = rows_out.shape[0]
    if count == l_ref.shape[0]:
        rows_out[...] = l_ref[...]
    else:
        rows_out[...] = l_ref[pl.ds(pl.multiple_of(place_ref[0] * count, count), count), :]
    wh[...], wl[...] = split(m_ref[...])
    copies = [
        pltpu.make_async_copy(x, y, sems.at[i])
        for i, (x, y) in enumerate(zip((rows_out, wh, wl), results))
    ]
    for copy in copies:
        copy.start()
    for copy in copies:
        copy.wait()


def factor_parts(size):
    square = shape(size, size)
    scratch = [pltpu.VMEM((LANES, LANES), jnp.float32)]
    vmem = pl.BlockSpec(memory_space=pltpu.VMEM)
    smem = pl.BlockSpec(memory_space=pltpu.SMEM)

    def first(place, pieces):
        return pl.pallas_call(
            first_kernel,
            out_shape=(square, square),
            in_specs=[smem] + [vmem] * len(pieces),
            out_specs=(vmem, vmem),
            scratch_shapes=scratch,
            name="factor_first",
        )(place, *pieces)

    def second(low, m):
        return pl.pallas_call(
            second_kernel,
            out_shape=(square, square),
            in_specs=[vmem, vmem],
            out_specs=(vmem, vmem),
            scratch_shapes=scratch,
            name="factor_second",
        )(low, m)

    def third(place, low, m, count):
        results = (shape(count, size),) + pair_shape(size, size)
        return pl.pallas_call(
            third_kernel,
            out_shape=results,
            in_specs=[smem, vmem, vmem],
            out_specs=(pl.BlockSpec(memory_space=pltpu.HBM),) * len(results),
            scratch_shapes=[pltpu.VMEM(x.shape, x.dtype) for x in results]
            + [pltpu.VMEM((size, size), jnp.float32)] * 2
            + scratch
            + [pltpu.SemaphoreType.DMA((len(results),))],
            name="factor_third",
        )(place, low, m)

    return first, second, third


NT = ((1,), (1,))
NN = ((1,), (0,))
TN = ((0,), (0,))


def split(x):
    high = x.astype(jnp.bfloat16)
    return high, (x - high.astype(jnp.float32)).astype(jnp.bfloat16)


def product(a, b, dims):
    def one(x, y):
        return lax.dot_general(x, y, (dims, ((), ())), preferred_element_type=jnp.float32)

    return one(a[0], b[0]) + (one(a[0], b[1]) + one(a[1], b[0]))


def shape(*dims, dtype=jnp.float32):
    return jax.ShapeDtypeStruct(dims, dtype)


def pair_shape(*dims):
    return (shape(*dims, dtype=jnp.bfloat16),) * 2


def in_hbm(x):
    return pltpu.with_memory_space_constraint(x, pltpu.HBM)


def full(*dims):
    return pl.BlockSpec(dims, lambda i, *_: (0,) * len(dims))


def tiles(*dims):
    return pl.BlockSpec(dims, lambda i, *_: (i,) + (0,) * (len(dims) - 1))


def run(kernel, grid, in_specs, out_specs, out_shape, scratch=(), prefetch=0, alias={}):
    return pl.pallas_call(
        kernel,
        grid_spec=pltpu.PrefetchScalarGridSpec(
            num_scalar_prefetch=prefetch,
            grid=(grid,),
            in_specs=in_specs,
            out_specs=out_specs,
            scratch_shapes=list(scratch),
        ),
        out_shape=out_shape,
        input_output_aliases=alias,
        compiler_params=pltpu.CompilerParams(vmem_limit_bytes=48 << 20),
    )


def columns(cross, inverse, tile):
    count, pw = cross.shape

    def kernel(c_ref, wh, wl, o_ref, oh_ref, ol_ref):
        out = lower_nt(split(c_ref[...]), (wh, wl))
        o_ref[...] = out
        oh_ref[...], ol_ref[...] = split(out)

    return run(
        kernel,
        count // tile,
        [tiles(tile, pw)] + [full(pw, pw)] * 2,
        (tiles(tile, pw),) * 3,
        (shape(count, pw),) + (pltpu.HBM((count, pw), jnp.bfloat16),) * 2,
    )(cross, *inverse)


def lower_nt(x, w_refs):
    pw = w_refs[0].shape[0]
    h = pw // 2
    top = product((x[0][:, :h], x[1][:, :h]), tuple(w[:h, :h] for w in w_refs), NT)
    low = product(x, tuple(w[h:, :] for w in w_refs), NT)
    return jnp.concatenate([top, low], 1)


def lower_nn(x, w_refs):
    pw = w_refs[0].shape[0]
    h = pw // 2
    left = product(x, tuple(w[:, :h] for w in w_refs), NN)
    right = product((x[0][:, h:], x[1][:, h:]), tuple(w[h:, h:] for w in w_refs), NN)
    return jnp.concatenate([left, right], 1)


def placed(flag_ref, masks, refs, out_refs):
    for m, x in zip(masks, refs):
        if isinstance(x, tuple):
            value = jnp.where(flag_ref[2] != 0, x[0][...], x[1][...])
        else:
            value = x[...]
        size = value.shape[0]
        span = pl.ds(pl.multiple_of((flag_ref[0] ^ m) * size, size), size)
        for out, part in zip(out_refs, split(value)):
            out[span, :] = part


def rows(picks, crosses, inverse, own, trail, tile):
    count, pw = crosses[0].shape
    total, width = trail.shape
    steps = count // tile

    def kernel(pick_ref, *refs):
        choices, (wh, wl, oh, ol, t_ref, out_ref, ch_ref, cl_ref) = (
            refs[: len(crosses)],
            refs[len(crosses) :],
        )
        pick = pick_ref[pl.program_id(0) // steps]
        x = choices[0][...]
        for i in range(1, len(choices)):
            x = jnp.where(pick == i, choices[i][...], x)
        r = split(lower_nt(split(x), (wh, wl)))
        out_ref[...] = t_ref[...] - product(r, (oh[...], ol[...]), NT)
        ch_ref[...], cl_ref[...] = split(lower_nn(r, (wh, wl)))

    def side(which):
        return pl.BlockSpec(
            (tile, pw), lambda i, p: (jnp.where(p[i // steps] == which, i % steps, 0), 0)
        )

    return run(
        kernel,
        total // tile,
        [side(k) for k in range(len(crosses))]
        + [full(pw, pw)] * 2
        + [full(*own[0].shape)] * 2
        + [tiles(tile, width)],
        (tiles(tile, width), tiles(tile, pw), tiles(tile, pw)),
        (shape(total, width),) + (pltpu.HBM((total, pw), jnp.bfloat16),) * 2,
        prefetch=1,
    )(picks, *crosses, *inverse, *own, trail)


def flatten(pieces):
    return [x for p in pieces for x in (p if isinstance(p, tuple) else (p,))]


def regroup(pieces, refs):
    it = iter(refs)
    return [(next(it), next(it)) if isinstance(p, tuple) else next(it) for p in pieces]


def maps(flags, masks, pieces, sectors, inverse, own, coupling, base, trail, tile):
    total, width = base.shape
    arrays = flatten(pieces)
    pw = inverse[0].shape[0]
    steps = total // tile
    own_rows, own_width = trail.shape
    own_tile, cut = own_rows // steps, width // steps
    n, k = len(arrays), len(sectors)

    def kernel(flag_ref, *refs):
        parts, sector_parts, refs = refs[:n], refs[n : n + k], refs[n + k :]
        wh, wl, oh, ol, ch, cl, b_ref, t_ref = refs[:8]
        out_ref, sec_ref, pred_ref, ph, plow, sh, sl, kh, kl = refs[8:]
        i = pl.program_id(0)

        @pl.when(i == 0)
        def _():
            placed(flag_ref, masks, regroup(pieces, parts), (ph, plow))
            placed(flag_ref, masks, sector_parts, (sh, sl))
            pair = (wh[...], wl[...])
            solved = split(product(pair, (sh[...], sl[...]), NN))
            sh[...], sl[...] = solved
            kh[...], kl[...] = split(product(pair, solved, TN))

        out_ref[...] = b_ref[...] - product((ch[...], cl[...]), (ph[...], plow[...]), NN)
        sec_ref[...] = t_ref[...] - product((oh[...], ol[...]), (sh[...], sl[...]), NN)
        span = pl.ds(pl.multiple_of(i * cut, cut), cut)
        pred_ref[...] = product((ph[:, span], plow[:, span]), (kh[...], kl[...]), TN)

    return run(
        kernel,
        steps,
        [full(*x.shape) for x in arrays + list(sectors)]
        + [full(pw, pw)] * 2
        + [tiles(own_tile, pw)] * 2
        + [tiles(tile, pw)] * 2
        + [tiles(tile, width), tiles(own_tile, own_width)],
        (tiles(tile, width), tiles(own_tile, own_width), tiles(cut, own_width)),
        (shape(total, width), shape(own_rows, own_width), shape(width, own_width)),
        scratch=[pltpu.VMEM((pw, width), jnp.bfloat16)] * 2
        + [pltpu.VMEM((pw, own_width), jnp.bfloat16)] * 4,
        prefetch=1,
    )(flags, *arrays, *sectors, *inverse, *own, *coupling, base, trail)


def exchange(x, axis, size, mask):
    return lax.ppermute(x, axis, [(i, i ^ mask) for i in range(size)])


def update(
    panel_block, panel_cross, trail_block, panel_pixels, trail_pixels, panel_sectors, trail_sectors
):
    n_row = lax.axis_size("row")
    n_col = lax.axis_size("col")
    r = lax.axis_index("row")
    c = lax.axis_index("col")
    count, pw = panel_block.shape
    owners = n_col // n_row
    first, second, third = factor_parts(pw)
    forward = n_row == 4
    masks = [0, 2, 1, 3] if forward else list(range(n_row))

    stack = [panel_block] + [exchange(panel_block, "row", n_row, m) for m in range(1, n_row)]
    stack = jnp.stack(stack)
    even = [stack] + [exchange(stack, "col", n_col, m) for m in range(2, n_col, 2)]
    odd = [exchange(x, "col", n_col, 1) for x in even]
    pieces = [x for pair in zip(even, odd) for x in pair]
    if count % SUBLANES:
        whole = jnp.stack(pieces)[jnp.arange(n_col) ^ c][:, jnp.arange(n_row) ^ r]
        whole = whole.transpose(1, 0, 2, 3).reshape(1, 1, pw, pw)
        pieces = [whole[0]]
        place = jnp.zeros((2,), jnp.int32)
    else:
        place = jnp.stack([r, c]).astype(jnp.int32)

    width = panel_sectors.shape[1] // n_row
    cuts = [
        lax.dynamic_slice_in_dim(panel_sectors, (r ^ m) * width, width, 1) for m in masks
    ]
    sector_pieces = [exchange(x, "row", n_row, m) if m else x for x, m in zip(cuts, masks)]
    if forward:
        near = exchange(panel_pixels, "row", n_row, 1)
        two = exchange(panel_pixels, "row", n_row, 2)
        middle = lax.ppermute(panel_pixels, "row", [(1, 2), (2, 1)])
    else:
        pixel_pieces = [
            exchange(panel_pixels, "row", n_row, m) if m else panel_pixels for m in masks
        ]

    low, m = first(place, pieces)
    bits = n_col.bit_length() - 1
    parity = c % 2
    held = panel_cross
    orders = [[1 + (s + j) % (bits - 1) for s in range(bits - 1)] for j in range(owners)]
    reached = [[0] for _ in range(owners)]
    early = bits == 3
    for s in range(bits - 1):
        pairs = []
        receives = jnp.zeros((), jnp.bool_)
        for j in range(owners):
            bit = 1 << orders[j][s]
            for i in range(n_row):
                base = i * owners + j
                pairs += [(i * n_col + (base ^ x), i * n_col + (base ^ x ^ bit)) for x in reached[j]]
            for x in reached[j]:
                receives |= c == ((r * owners + j) ^ x ^ bit)
            reached[j] += [x ^ bit for x in reached[j]]
        got = lax.ppermute(held, ("row", "col"), pairs)
        if early and s == bits - 2:
            break
        held = jnp.where(receives, got, held)
    if early:
        beside = exchange(held, "col", n_col, 1)
        last = exchange(got, "col", n_col, 1)
        seat = c ^ (r * owners)
        source = seat < 2
        holder = source | (seat == (1 << orders[0][0])) | (seat == ((1 << orders[1][0]) | 1))
        mate = (seat == ((1 << orders[0][0]) | 1)) | (seat == (1 << orders[1][0]))
        crosses = [held, beside, got, last]
        kept = jnp.where(holder, 0, 2)
        swapped = jnp.where(source, 1, jnp.where(mate, 1, 3))
    else:
        crosses = [held, exchange(held, "col", n_col, 1)]
        kept, swapped = 0 * c, 0 * c + 1
    ints = lambda *v: jnp.stack([jnp.asarray(x, jnp.int32) for x in v])
    picks = ints(
        jnp.where(parity == 0, kept, swapped),
        jnp.where(parity == 0, swapped, kept),
    )

    whole_rows = count % SUBLANES != 0
    low, m = second(low, m)
    if forward:
        far = lax.ppermute(two, "row", [(1, 0), (2, 3)])
        pixel_pieces = [panel_pixels, two, near, (middle, far)]
    factor_rows, *inverse = third(ints(r * n_col + c), low, m, pw if whole_rows else count)
    inverse = [in_hbm(x) for x in inverse]
    column_own, *own = columns(panel_cross, inverse, min(256, panel_cross.shape[0]))
    own = [in_hbm(x) for x in own]
    if whole_rows:
        factor_rows = lax.dynamic_slice_in_dim(factor_rows, (r * n_col + c) * count, count, 0)
    tile = min(512, panel_cross.shape[0])
    trail_updated, *coupling = rows(picks, crosses, inverse, own, trail_block, tile)
    coupling = [in_hbm(x) for x in coupling]
    flags = ints(r, 0, (r == 1) | (r == 2))
    pixel_total, sectors_updated, predicted = maps(
        flags, masks, pixel_pieces, sector_pieces, inverse, own, coupling,
        trail_pixels, trail_sectors, tile,
    )
    return (factor_rows, column_own, trail_updated, pixel_total, sectors_updated, predicted)


def solution(mesh):
    return jax.shard_map(
        update,
        mesh=mesh,
        in_specs=(
            P(("row", "col"), None),
            P("col", None),
            P("row", "col"),
            P("row", "col"),
            P("row", "col"),
            P("row", None),
            P("col", "row"),
        ),
        out_specs=(
            P(("row", "col"), None),
            P("col", None),
            P("row", "col"),
            P("row", "col"),
            P("col", "row"),
            P("col", "row"),
        ),
        check_vma=False,
    )
```

```python
import jax
import jax.numpy as jnp
from jax import lax
from jax.experimental import pallas as pl
from jax.experimental.pallas import tpu as pltpu
from jax.sharding import PartitionSpec as P


HIGHEST = lax.Precision.HIGHEST
LANES = 128
SUBLANES = 8


def invert_block(tiles):
    count = len(tiles)
    width = tiles[0].shape[1]
    shape = (SUBLANES, width)
    lane = lax.broadcasted_iota(jnp.int32, shape, 1)
    sub = lax.broadcasted_iota(jnp.int32, shape, 0)

    def lanes_of(x, j):
        return jnp.broadcast_to(x[:, j : j + 1], shape)

    def row_of(x, i):
        return jnp.broadcast_to(x[i : i + 1, :], shape)

    m = list(tiles)
    out = []
    for g in range(count):
        base = SUBLANES * g
        inside = (lane >= base) & (lane < base + SUBLANES)
        columns = [[lanes_of(m[v], base + q) for q in range(SUBLANES)] for v in range(g, count)]
        s = [
            [row_of(columns[0][q], i) if i >= q else None for q in range(SUBLANES)]
            for i in range(SUBLANES)
        ]
        low = [[None] * SUBLANES for _ in range(SUBLANES)]
        pivot_inv = []
        root_inv = []
        for q in range(SUBLANES):
            pivot_inv.append(1.0 / s[q][q])
            root_inv.append(lax.rsqrt(s[q][q]))
            for i in range(q + 1, SUBLANES):
                low[i][q] = s[i][q] * pivot_inv[q]
            for i in range(q + 1, SUBLANES):
                for k in range(q + 1, i + 1):
                    s[i][k] = s[i][k] - low[i][q] * s[k][q]
        rows = []
        for q in range(SUBLANES):
            x = jnp.where(inside, jnp.where(lane == base + q, 1.0, 0.0), row_of(m[g], q))
            for p in range(q):
                x = x - low[q][p] * rows[p]
            rows.append(x)
        own = jnp.zeros(shape, jnp.float32)
        for q in range(SUBLANES):
            own = jnp.where((sub == q) & (lane <= base + q), rows[q] * root_inv[q], own)
        out.append(own)
        for v in range(g + 1, count):
            done = []
            for q in range(SUBLANES):
                x = columns[v - g][q]
                for p in range(q):
                    x = x - done[p] * low[q][p]
                done.append(x)
            x = jnp.where(inside, 0.0, m[v])
            for q in range(SUBLANES):
                x = x - (done[q] * pivot_inv[q]) * rows[q]
            m[v] = x
    return out


def factor_step(k, m_ref, l_ref, wk_ref):
    size = m_ref.shape[0]
    width = wk_ref.shape[0]
    offset = k * width if isinstance(k, int) else pl.multiple_of(k * width, width)
    span = pl.ds(offset, width)
    block = m_ref.at[span, span]
    tiles = [block[i : i + SUBLANES, :] for i in range(0, width, SUBLANES)]
    for i, tile in enumerate(invert_block(tiles)):
        wk_ref[i * SUBLANES : (i + 1) * SUBLANES, :] = tile
    inverse = wk_ref[...]
    start = offset if isinstance(k, int) else 0
    panel = lax.dot_general(
        m_ref[start:, span],
        inverse,
        (((1,), (1,)), ((), ())),
        precision=HIGHEST,
        preferred_element_type=jnp.float32,
    )
    row = lax.broadcasted_iota(jnp.int32, (size - start, width), 0) + start
    col = lax.broadcasted_iota(jnp.int32, (size - start, width), 1) + offset
    below = row >= offset + width
    l_ref[start:, span] = jnp.where(row >= col, panel, 0.0)
    ii = lax.broadcasted_iota(jnp.int32, (width, width), 0)
    jj = lax.broadcasted_iota(jnp.int32, (width, width), 1)
    m_ref[span, span] = jnp.where(ii == jj, 1.0, 0.0)
    upper = jnp.dot(inverse, m_ref[span, :], precision=HIGHEST, preferred_element_type=jnp.float32)
    lane = lax.broadcasted_iota(jnp.int32, (width, size), 1)
    if isinstance(k, int):
        start += width
        panel = panel[width:, :]
        m_ref[:, span] = jnp.zeros((size, width), jnp.float32)
    else:
        m_ref[:, span] = jnp.where(below, 0.0, m_ref[:, span])
        panel = jnp.where(below, panel, 0.0)
    if start < size:
        m_ref[start:, :] = m_ref[start:, :] - jnp.dot(
            panel, upper, precision=HIGHEST, preferred_element_type=jnp.float32
        )
    m_ref[span, :] = jnp.where(lane < offset + width, upper, 0.0)


def first_kernel(place_ref, *refs):
    pieces, (l_ref, m_ref, wk_ref) = refs[:-3], refs[-3:]
    n_row, count, _ = pieces[0].shape
    for t, piece in enumerate(pieces):
        for m in range(n_row):
            slot = (place_ref[0] ^ m) * len(pieces) + (place_ref[1] ^ t)
            m_ref[pl.ds(pl.multiple_of(slot * count, count), count), :] = piece[m]
    l_ref[...] = jnp.zeros_like(l_ref)

    @pl.loop(0, m_ref.shape[0] // wk_ref.shape[0] // 2)
    def _(k):
        factor_step(k, m_ref, l_ref, wk_ref)


def second_kernel(l_in, m_in, l_ref, m_ref, wk_ref):
    l_ref[...] = l_in[...]
    m_ref[...] = m_in[...]
    blocks = m_ref.shape[0] // wk_ref.shape[0]

    for k in range(blocks // 2, blocks - 1):
        factor_step(k, m_ref, l_ref, wk_ref)


def third_kernel(place_ref, l_in, m_in, *refs):
    results, (rows_out, wh, wl), (l_ref, m_ref, wk_ref, sems) = refs[:3], refs[3:6], refs[6:]
    l_ref[...] = l_in[...]
    m_ref[...] = m_in[...]
    factor_step(m_ref.shape[0] // wk_ref.shape[0] - 1, m_ref, l_ref, wk_ref)
    count = rows_out.shape[0]
    if count == l_ref.shape[0]:
        rows_out[...] = l_ref[...]
    else:
        rows_out[...] = l_ref[pl.ds(pl.multiple_of(place_ref[0] * count, count), count), :]
    wh[...], wl[...] = split(m_ref[...])
    copies = [
        pltpu.make_async_copy(x, y, sems.at[i])
        for i, (x, y) in enumerate(zip((rows_out, wh, wl), results))
    ]
    for copy in copies:
        copy.start()
    for copy in copies:
        copy.wait()


def factor_parts(size):
    square = shape(size, size)
    scratch = [pltpu.VMEM((LANES, LANES), jnp.float32)]
    vmem = pl.BlockSpec(memory_space=pltpu.VMEM)
    smem = pl.BlockSpec(memory_space=pltpu.SMEM)

    def first(place, pieces):
        return pl.pallas_call(
            first_kernel,
            out_shape=(square, square),
            in_specs=[smem] + [vmem] * len(pieces),
            out_specs=(vmem, vmem),
            scratch_shapes=scratch,
            name="factor_first",
        )(place, *pieces)

    def second(low, m):
        return pl.pallas_call(
            second_kernel,
            out_shape=(square, square),
            in_specs=[vmem, vmem],
            out_specs=(vmem, vmem),
            scratch_shapes=scratch,
            name="factor_second",
        )(low, m)

    def third(place, low, m, count):
        results = (shape(count, size),) + pair_shape(size, size)
        return pl.pallas_call(
            third_kernel,
            out_shape=results,
            in_specs=[smem, vmem, vmem],
            out_specs=(pl.BlockSpec(memory_space=pltpu.HBM),) * len(results),
            scratch_shapes=[pltpu.VMEM(x.shape, x.dtype) for x in results]
            + [pltpu.VMEM((size, size), jnp.float32)] * 2
            + scratch
            + [pltpu.SemaphoreType.DMA((len(results),))],
            name="factor_third",
        )(place, low, m)

    return first, second, third


NT = ((1,), (1,))
NN = ((1,), (0,))
TN = ((0,), (0,))


def split(x):
    high = x.astype(jnp.bfloat16)
    return high, (x - high.astype(jnp.float32)).astype(jnp.bfloat16)


def product(a, b, dims):
    def one(x, y):
        return lax.dot_general(x, y, (dims, ((), ())), preferred_element_type=jnp.float32)

    return one(a[0], b[0]) + (one(a[0], b[1]) + one(a[1], b[0]))


def shape(*dims, dtype=jnp.float32):
    return jax.ShapeDtypeStruct(dims, dtype)


def pair_shape(*dims):
    return (shape(*dims, dtype=jnp.bfloat16),) * 2


def in_hbm(x):
    return pltpu.with_memory_space_constraint(x, pltpu.HBM)


def full(*dims):
    return pl.BlockSpec(dims, lambda i, *_: (0,) * len(dims))


def tiles(*dims):
    return pl.BlockSpec(dims, lambda i, *_: (i,) + (0,) * (len(dims) - 1))


def run(kernel, grid, in_specs, out_specs, out_shape, scratch=(), prefetch=0, alias={}):
    return pl.pallas_call(
        kernel,
        grid_spec=pltpu.PrefetchScalarGridSpec(
            num_scalar_prefetch=prefetch,
            grid=(grid,),
            in_specs=in_specs,
            out_specs=out_specs,
            scratch_shapes=list(scratch),
        ),
        out_shape=out_shape,
        input_output_aliases=alias,
        compiler_params=pltpu.CompilerParams(vmem_limit_bytes=48 << 20),
    )


def columns(cross, inverse, tile):
    count, pw = cross.shape

    def kernel(c_ref, wh, wl, o_ref, oh_ref, ol_ref):
        out = lower_nt(split(c_ref[...]), (wh, wl))
        o_ref[...] = out
        oh_ref[...], ol_ref[...] = split(out)

    return run(
        kernel,
        count // tile,
        [tiles(tile, pw)] + [full(pw, pw)] * 2,
        (tiles(tile, pw),) * 3,
        (shape(count, pw),) + (pltpu.HBM((count, pw), jnp.bfloat16),) * 2,
    )(cross, *inverse)


def lower_nt(x, w_refs):
    pw = w_refs[0].shape[0]
    h = pw // 2
    top = product((x[0][:, :h], x[1][:, :h]), tuple(w[:h, :h] for w in w_refs), NT)
    low = product(x, tuple(w[h:, :] for w in w_refs), NT)
    return jnp.concatenate([top, low], 1)


def lower_nn(x, w_refs):
    pw = w_refs[0].shape[0]
    h = pw // 2
    left = product(x, tuple(w[:, :h] for w in w_refs), NN)
    right = product((x[0][:, h:], x[1][:, h:]), tuple(w[h:, h:] for w in w_refs), NN)
    return jnp.concatenate([left, right], 1)


def placed(flag_ref, masks, refs, out_refs):
    for m, x in zip(masks, refs):
        if isinstance(x, tuple):
            value = jnp.where(flag_ref[2] != 0, x[0][...], x[1][...])
        else:
            value = x[...]
        size = value.shape[0]
        span = pl.ds(pl.multiple_of((flag_ref[0] ^ m) * size, size), size)
        for out, part in zip(out_refs, split(value)):
            out[span, :] = part


def rows(picks, crosses, inverse, own, trail, tile):
    count, pw = crosses[0].shape
    total, width = trail.shape
    steps = count // tile

    n = len(crosses)

    def kernel(pick_ref, *refs):
        choices, refs = refs[:n], refs[n:]
        wh, wl, oh, ol, t_ref, out_ref, ch_ref, cl_ref, x_ref, sems = refs
        i = pl.program_id(0)

        def take(k, source, j, target):
            return pltpu.make_async_copy(
                choices[k].at[pl.ds(source, tile)], x_ref.at[pl.ds(target, tile)], sems.at[j]
            )

        @pl.when(i == 0)
        def _():
            for j in range(total // tile):
                for k in range(n):

                    @pl.when(pick_ref[j // steps] == k)
                    def _():
                        take(k, (j % steps) * tile, j, j * tile).start()

        place = pl.multiple_of(i * tile, tile)
        take(0, 0, i, place).wait()
        x = x_ref[pl.ds(place, tile), :]
        r = split(lower_nt(split(x), (wh, wl)))
        out_ref[...] = t_ref[...] - product(r, (oh[...], ol[...]), NT)
        ch_ref[...], cl_ref[...] = split(lower_nn(r, (wh, wl)))

    return run(
        kernel,
        total // tile,
        [pl.BlockSpec(memory_space=pl.ANY)] * n
        + [full(pw, pw)] * 2
        + [full(*own[0].shape)] * 2
        + [tiles(tile, width)],
        (tiles(tile, width), tiles(tile, pw), tiles(tile, pw)),
        (shape(total, width),) + (pltpu.HBM((total, pw), jnp.bfloat16),) * 2,
        scratch=[
            pltpu.VMEM((total, pw), jnp.float32),
            pltpu.SemaphoreType.DMA((total // tile,)),
        ],
        prefetch=1,
    )(picks, *crosses, *inverse, *own, trail)


def flatten(pieces):
    return [x for p in pieces for x in (p if isinstance(p, tuple) else (p,))]


def regroup(pieces, refs):
    it = iter(refs)
    return [(next(it), next(it)) if isinstance(p, tuple) else next(it) for p in pieces]


def maps(flags, masks, pieces, sectors, inverse, own, coupling, base, trail, tile):
    total, width = base.shape
    arrays = flatten(pieces)
    pw = inverse[0].shape[0]
    steps = total // tile
    own_rows, own_width = trail.shape
    own_tile, cut = own_rows // steps, width // steps
    n, k = len(arrays), len(sectors)

    def kernel(flag_ref, *refs):
        parts, sector_parts, refs = refs[:n], refs[n : n + k], refs[n + k :]
        wh, wl, oh, ol, ch, cl, b_ref, t_ref = refs[:8]
        out_ref, sec_ref, pred_ref, ph, plow, sh, sl, kh, kl = refs[8:]
        i = pl.program_id(0)

        @pl.when(i == 0)
        def _():
            placed(flag_ref, masks, regroup(pieces, parts), (ph, plow))
            placed(flag_ref, masks, sector_parts, (sh, sl))
            pair = (wh[...], wl[...])
            solved = split(product(pair, (sh[...], sl[...]), NN))
            sh[...], sl[...] = solved
            kh[...], kl[...] = split(product(pair, solved, TN))

        out_ref[...] = b_ref[...] - product((ch[...], cl[...]), (ph[...], plow[...]), NN)
        sec_ref[...] = t_ref[...] - product((oh[...], ol[...]), (sh[...], sl[...]), NN)
        span = pl.ds(pl.multiple_of(i * cut, cut), cut)
        pred_ref[...] = product((ph[:, span], plow[:, span]), (kh[...], kl[...]), TN)

    return run(
        kernel,
        steps,
        [full(*x.shape) for x in arrays + list(sectors)]
        + [full(pw, pw)] * 2
        + [tiles(own_tile, pw)] * 2
        + [tiles(tile, pw)] * 2
        + [tiles(tile, width), tiles(own_tile, own_width)],
        (tiles(tile, width), tiles(own_tile, own_width), tiles(cut, own_width)),
        (shape(total, width), shape(own_rows, own_width), shape(width, own_width)),
        scratch=[pltpu.VMEM((pw, width), jnp.bfloat16)] * 2
        + [pltpu.VMEM((pw, own_width), jnp.bfloat16)] * 4,
        prefetch=1,
    )(flags, *arrays, *sectors, *inverse, *own, *coupling, base, trail)


def exchange(x, axis, size, mask):
    return lax.ppermute(x, axis, [(i, i ^ mask) for i in range(size)])


def update(
    panel_block, panel_cross, trail_block, panel_pixels, trail_pixels, panel_sectors, trail_sectors
):
    n_row = lax.axis_size("row")
    n_col = lax.axis_size("col")
    r = lax.axis_index("row")
    c = lax.axis_index("col")
    count, pw = panel_block.shape
    owners = n_col // n_row
    first, second, third = factor_parts(pw)
    forward = n_row == 4
    masks = [0, 2, 1, 3] if forward else list(range(n_row))

    stack = [panel_block] + [exchange(panel_block, "row", n_row, m) for m in range(1, n_row)]
    stack = jnp.stack(stack)
    even = [stack] + [exchange(stack, "col", n_col, m) for m in range(2, n_col, 2)]
    odd = [exchange(x, "col", n_col, 1) for x in even]
    pieces = [x for pair in zip(even, odd) for x in pair]
    if count % SUBLANES:
        whole = jnp.stack(pieces)[jnp.arange(n_col) ^ c][:, jnp.arange(n_row) ^ r]
        whole = whole.transpose(1, 0, 2, 3).reshape(1, 1, pw, pw)
        pieces = [whole[0]]
        place = jnp.zeros((2,), jnp.int32)
    else:
        place = jnp.stack([r, c]).astype(jnp.int32)

    width = panel_sectors.shape[1] // n_row
    cuts = [
        lax.dynamic_slice_in_dim(panel_sectors, (r ^ m) * width, width, 1) for m in masks
    ]
    sector_pieces = [exchange(x, "row", n_row, m) if m else x for x, m in zip(cuts, masks)]
    if forward:
        near = exchange(panel_pixels, "row", n_row, 1)
        two = exchange(panel_pixels, "row", n_row, 2)
        middle = lax.ppermute(panel_pixels, "row", [(1, 2), (2, 1)])
    else:
        pixel_pieces = [
            exchange(panel_pixels, "row", n_row, m) if m else panel_pixels for m in masks
        ]

    low, m = first(place, pieces)
    bits = n_col.bit_length() - 1
    parity = c % 2
    held = panel_cross
    orders = [[1 + (s + j) % (bits - 1) for s in range(bits - 1)] for j in range(owners)]
    reached = [[0] for _ in range(owners)]
    early = bits == 3
    for s in range(bits - 1):
        pairs = []
        receives = jnp.zeros((), jnp.bool_)
        for j in range(owners):
            bit = 1 << orders[j][s]
            for i in range(n_row):
                base = i * owners + j
                pairs += [(i * n_col + (base ^ x), i * n_col + (base ^ x ^ bit)) for x in reached[j]]
            for x in reached[j]:
                receives |= c == ((r * owners + j) ^ x ^ bit)
            reached[j] += [x ^ bit for x in reached[j]]
        got = lax.ppermute(held, ("row", "col"), pairs)
        if early and s == bits - 2:
            break
        held = jnp.where(receives, got, held)
    if early:
        beside = exchange(held, "col", n_col, 1)
        last = exchange(got, "col", n_col, 1)
        seat = c ^ (r * owners)
        source = seat < 2
        holder = source | (seat == (1 << orders[0][0])) | (seat == ((1 << orders[1][0]) | 1))
        mate = (seat == ((1 << orders[0][0]) | 1)) | (seat == (1 << orders[1][0]))
        crosses = [held, beside, got, last]
        kept = jnp.where(holder, 0, 2)
        swapped = jnp.where(source, 1, jnp.where(mate, 1, 3))
    else:
        crosses = [held, exchange(held, "col", n_col, 1)]
        kept, swapped = 0 * c, 0 * c + 1
    ints = lambda *v: jnp.stack([jnp.asarray(x, jnp.int32) for x in v])
    picks = ints(
        jnp.where(parity == 0, kept, swapped),
        jnp.where(parity == 0, swapped, kept),
    )

    whole_rows = count % SUBLANES != 0
    low, m = second(low, m)
    if forward:
        far = lax.ppermute(two, "row", [(1, 0), (2, 3)])
        pixel_pieces = [panel_pixels, two, near, (middle, far)]
    factor_rows, *inverse = third(ints(r * n_col + c), low, m, pw if whole_rows else count)
    inverse = [in_hbm(x) for x in inverse]
    column_own, *own = columns(panel_cross, inverse, min(256, panel_cross.shape[0]))
    own = [in_hbm(x) for x in own]
    if whole_rows:
        factor_rows = lax.dynamic_slice_in_dim(factor_rows, (r * n_col + c) * count, count, 0)
    tile = min(512, panel_cross.shape[0])
    trail_updated, *coupling = rows(picks, crosses, inverse, own, trail_block, tile)
    coupling = [in_hbm(x) for x in coupling]
    flags = ints(r, 0, (r == 1) | (r == 2))
    pixel_total, sectors_updated, predicted = maps(
        flags, masks, pixel_pieces, sector_pieces, inverse, own, coupling,
        trail_pixels, trail_sectors, tile,
    )
    return (factor_rows, column_own, trail_updated, pixel_total, sectors_updated, predicted)


def solution(mesh):
    return jax.shard_map(
        update,
        mesh=mesh,
        in_specs=(
            P(("row", "col"), None),
            P("col", None),
            P("row", "col"),
            P("row", "col"),
            P("row", "col"),
            P("row", None),
            P("col", "row"),
        ),
        out_specs=(
            P(("row", "col"), None),
            P("col", None),
            P("row", "col"),
            P("row", "col"),
            P("col", "row"),
            P("col", "row"),
        ),
        check_vma=False,
    )
```
